128 devices in a mesh: grp: 4 (over x), vid: 32 (over y, z, core).
Axes of the slice: x: 4, y: 4, z: 4, core: 2. Of those that a mesh axis runs over, the one named last changes fastest.
Arguments:
- frames: bfloat16 [131072, 1024], P(('grp', 'vid')), parts along dimension 0, may hold values from -240 to 240
- w_frame: bfloat16 [1024, 512], replicated, may hold values from -0.1875 to 0.1875
- step_emb: bfloat16 [16384, 512], P(('grp', 'vid')), parts along dimension 0, may hold values from -6 to 6
- targets: int32 [131072], P(('grp', 'vid')), parts along dimension 0, may hold values from 0 to 127
- tile_frame: int32 [128, 128], P(('grp', 'vid')), parts along dimension 0, may hold values from 0 to 7, as said below
- tile_step: int32 [128, 128], P(('grp', 'vid')), parts along dimension 0, may hold values from 0 to 31, as said below
- tile_count: int32 [128], P(('grp', 'vid')), parts along dimension 0, may hold values from 8 to 128, as said below
Outputs:
- row_loss: float32 [131072], P(('grp', 'vid')), parts along dimension 0
- frame_grad: bfloat16 [131072, 1024], P(('grp', 'vid')), parts along dimension 0
- step_grad: float32 [16384, 512], P(('grp', 'vid')), parts along dimension 0
The draws below stay inside these ranges and needn't reach their ends.
There are 4 independent parts, one for each index of `grp`. The reference program is written for one: setup_inputs(seed, part) draws one part's arguments, and reference() takes and returns one part's arrays. A program takes and returns all parts, laid end to end along the dimension named above; an argument that names none is the same for every part. Nothing has to cross between parts.
Inputs may be any that keep to these rules, and one draw needn't show every extreme that they name: `tile_frame`: each run of 8 tiles of a list, starting at a multiple of 8, names every frame block once. `tile_step`: the (frame block, step block) pairs of one video's list are distinct; the first 8 tiles pair each frame block with the video's own step block. Only the first tile_count tiles of a list are valid; some video's list is full.
All inputs are finite; a program needn't handle non-finite values.
Results may differ from the reference program's by a relative error of at most 0.0086.
Values may be sent and summed in bfloat16 or wider, within the bound.
A program may use at most 128 MiB of HBM per device.

```python
import math
import jax
import jax.numpy as jnp
from jax import lax

D = 1024
E = 512
S_DEV = 128
FR_DEV = 1024
MAXT = 128
FRAMES = 32768
STEPS = 4096
N_VID = 32


def draw_frames(key, part):
    first = jax.random.fold_in(key, 0)
    base = jax.random.normal(first, (FRAMES, D), jnp.float32)
    return jnp.clip(base, -240.0, 240.0).astype(jnp.bfloat16)


def tile_tables(key):
    inner = jax.random.fold_in(key, 7)
    count_key, perm_key, pick_key, order_key = jax.random.split(inner, 4)
    blocks = FR_DEV // 128
    rounds = MAXT // blocks
    keys = jax.random.split(perm_key, N_VID)
    perms = jax.vmap(lambda single: jax.random.permutation(single, N_VID - 1))(keys)
    order_keys = jax.random.split(order_key, N_VID * rounds)
    orders = jax.vmap(lambda single: jax.random.permutation(single, blocks))(order_keys)
    frame_tab = orders.reshape(N_VID, MAXT).astype(jnp.int32)
    slots = jnp.arange(MAXT, dtype=jnp.int32)
    round_of = slots // blocks
    column = (round_of[None, :] - 1 + frame_tab) % (N_VID - 1)
    videos = jnp.arange(N_VID, dtype=jnp.int32)[:, None]
    other = (videos + 1 + jnp.take_along_axis(perms, column, axis=1)) % N_VID
    step_of = jnp.where(round_of[None, :] == 0, videos, other).astype(jnp.int32)
    counts = jax.random.randint(count_key, (N_VID,), blocks, MAXT + 1)
    chosen = jax.random.randint(pick_key, (), 0, N_VID)
    counts = jnp.where(jnp.arange(N_VID) == chosen, MAXT, counts).astype(jnp.int32)
    return (frame_tab, step_of, counts)


def draw_tile_frame(key, part):
    return tile_tables(key)[0]


def draw_tile_step(key, part):
    return tile_tables(key)[1]


def draw_tile_count(key, part):
    return tile_tables(key)[2]


def with_ends(result, stream_key, least, top_value):
    spot = [jax.random.randint(jax.random.fold_in(stream_key, axis), (), 0, length) for axis, length in enumerate(result.shape)]
    widest = result.shape.index(max(result.shape))
    beside = spot[:widest] + [(spot[widest] + 1) % result.shape[widest]] + spot[widest + 1:]
    return result.at[tuple(spot)].set(least).at[tuple(beside)].set(top_value)


def steps_of(stream_key, dims, cuts, smallest, largest):
    level = 1.0
    for dim, parts in cuts:
        steps = jax.random.uniform(jax.random.fold_in(jax.random.fold_in(stream_key, 6), dim), (parts,), jnp.float32, smallest / len(cuts), largest / len(cuts))
        level = level * jnp.repeat(jnp.exp(steps), dims[dim] // parts).reshape((-1,) + (1,) * (len(dims) - 1 - dim))
    return level


def noise(rng, extent, deviation, limit, shards=(), kind=jnp.bfloat16):
    values = jax.random.normal(rng, extent, jnp.float32) * deviation
    if len(shards) > 0:
        values = steps_of(rng, extent, shards, -0.22, 0.18) * values
    return jnp.clip(values, min=-limit, max=limit).astype(kind)


def setup_inputs(seed: int = 0, part: int = 0) -> dict:
    seeds = jax.random.split(jax.random.key(seed), 8)
    part_keys = jax.random.split(jax.random.fold_in(seeds[7], part), 8)
    frames = draw_frames(jax.random.fold_in(jax.random.fold_in(seeds[7], part), 71), part)
    w_frame = noise(seeds[1], (D, E), D ** -0.5, 0.1875)
    step_emb = noise(part_keys[2], (STEPS, E), 1.0, 6.0, ((0, 32),))
    targets = with_ends(jax.random.randint(part_keys[3], (FRAMES,), 0, S_DEV), jax.random.fold_in(part_keys[3], 1), 0, S_DEV - 1).astype(jnp.int32)
    tile_frame = draw_tile_frame(jax.random.fold_in(jax.random.fold_in(seeds[7], part), 71), part)
    tile_step = draw_tile_step(jax.random.fold_in(jax.random.fold_in(seeds[7], part), 71), part)
    tile_count = draw_tile_count(jax.random.fold_in(jax.random.fold_in(seeds[7], part), 71), part)
    return dict(frames=frames, w_frame=w_frame, step_emb=step_emb, targets=targets, tile_frame=tile_frame, tile_step=tile_step, tile_count=tile_count)


def reference(frames, w_frame, step_emb, targets, tile_frame, tile_step, tile_count):
    width = step_emb.shape[1]
    temper = 1.0 / math.sqrt(width)
    blocks = FR_DEV // 128

    def per_video(carry, video):
        video = video.astype(jnp.int32)
        rows_v = lax.dynamic_slice_in_dim(frames, video * FR_DEV, FR_DEV)
        goals = lax.dynamic_slice_in_dim(targets, video * FR_DEV, FR_DEV)
        embedded = jnp.dot(rows_v, w_frame, preferred_element_type=jnp.float32).astype(jnp.bfloat16)
        valid = (jnp.arange(MAXT) < tile_count[video]).astype(jnp.int32)
        allowed = jnp.zeros((blocks, N_VID), jnp.int32).at[tile_frame[video], tile_step[video]].max(valid)
        wide = jnp.repeat(jnp.repeat(allowed, 128, axis=0), S_DEV, axis=1) > 0
        scores = jnp.dot(embedded, step_emb.T, preferred_element_type=jnp.float32) * temper
        top = lax.optimization_barrier(jnp.max(jnp.where(wide, scores, -jnp.inf), axis=1, keepdims=True))
        total = lax.optimization_barrier(jnp.sum(jnp.where(wide, jnp.exp(jnp.where(wide, scores - top, 0.0)), 0.0), axis=1, keepdims=True))
        lse = top + jnp.log(total)
        owners = (video * S_DEV + goals).astype(jnp.int32)
        chosen = step_emb[owners].astype(jnp.float32)
        positive = lax.optimization_barrier(jnp.sum(embedded.astype(jnp.float32) * chosen, axis=1)) * temper
        loss = lse[:, 0] - positive
        probs = jnp.where(wide, jnp.exp(jnp.where(wide, scores - lse, 0.0)), 0.0).astype(jnp.bfloat16)
        grad_rows = jnp.dot(probs, step_emb, preferred_element_type=jnp.float32) * temper - chosen * temper
        frame_grad = lax.dot_general(grad_rows.astype(jnp.bfloat16), w_frame, (((1,), (1,)), ((), ())), preferred_element_type=jnp.float32).astype(jnp.bfloat16)
        grad_cols = jnp.dot(probs.T, embedded, preferred_element_type=jnp.float32) * temper
        own_term = jax.ops.segment_sum(embedded.astype(jnp.float32) * temper, owners, num_segments=N_VID * S_DEV)
        return (carry + grad_cols - own_term, (loss, frame_grad))
    start = jnp.zeros((N_VID * S_DEV, width), jnp.float32)
    step_grad, (losses, grads) = lax.scan(per_video, start, jnp.arange(N_VID, dtype=jnp.int32))
    return (losses.reshape(-1), grads.reshape(-1, frames.shape[1]), step_grad)
```

```python
import functools
import math

import jax
import jax.numpy as jnp
from jax import lax
from jax.experimental import pallas as pl
from jax.experimental.pallas import tpu as pltpu
from jax.sharding import PartitionSpec as P

F32 = jnp.float32
BF16 = jnp.bfloat16
MESH = pl.DeviceIdType.MESH
NT = (((1,), (1,)), ((), ()))
SIDE = 4
CHIPS = SIDE * SIDE
BLK = 128
LOG2E = 1.0 / math.log(2.0)
LN2 = math.log(2.0)
FAR = -1e30

ORDER = [
    (0, 0), (0, 1), (1, 0), (0, 3), (3, 0), (1, 1), (3, 3), (1, 3),
    (3, 1), (2, 0), (0, 2), (2, 1), (1, 2), (2, 3), (3, 2), (2, 2),
]
POS = {place: k for k, place in enumerate(ORDER)}
TURN = [POS[(db, da)] for da, db in ORDER]

GATHER = {
    0: [(3, 0), (1, 0), (0, 3), (0, 1)],
    3: [(2, 0), (3, 3), (1, 1), (3, 1), (1, 3), (0, 2)],
    10: [(2, 1), (2, 3), (1, 2), (3, 2)],
    14: [(2, 2)],
}
ONWARD = {
    (0, 0): ["a+", "a-", "b+", "b-"],
    (3, 0): ["a+", "b+", "b-"],
    (1, 0): ["b+", "b-"],
    (2, 0): ["b+", "b-"],
    (0, 3): ["b+"],
    (1, 3): ["b+"],
    (2, 1): ["b-"],
    (3, 1): ["b-"],
}
SHIFT = {"a+": (-1, 0), "a-": (1, 0), "b+": (0, -1), "b-": (0, 1)}

LANDS = ["h0", "h1", "h2", "h3", "p0", "p1", "p2", "p3",
         "m0", "m1", "m2", "m3", "A", "Ap", "Am"]
LAND = {name: i for i, name in enumerate(LANDS)}
COMBINE = {
    (2, 2): ([], "b-", "h2"),
    (3, 2): ([], "b-", "h3"),
    (1, 2): ([], "b+", "h1"),
    (0, 2): ([], "b+", "h0"),
    (2, 3): (["h2"], "b-", "m2"),
    (3, 3): (["h3"], "b-", "m3"),
    (1, 3): ([], "b-", "m1"),
    (0, 3): ([], "b-", "m0"),
    (2, 1): ([], "b+", "p2"),
    (3, 1): ([], "b+", "p3"),
    (1, 1): (["h1"], "b+", "p1"),
    (0, 1): (["h0"], "b+", "p0"),
    (2, 0): (["p2", "m2"], "a+", "A"),
    (1, 0): (["p1", "m1", "A"], "a+", "Ap"),
    (3, 0): (["p3", "m3"], "a-", "Am"),
}
REDUCE = {
    1: [(2, 2)],
    3: [(3, 2)],
    4: [(2, 3)],
    5: [(2, 1), (1, 2)],
    7: [(0, 2)],
    8: [(2, 0)],
    9: [(1, 3), (3, 1)],
    10: [(3, 3)],
    11: [(1, 1)],
    13: [(3, 0), (0, 3)],
    14: [(0, 1)],
    15: [(1, 0)],
}


def kernel(
    step_in, tgt, tile_frame, tile_step, count, frames_hbm, w_hbm,
    loss, grad_hbm, step_grad,
    frames, w, emb, table, table_t, scores, probs, bias, top, total, shift,
    onehot, own, part, side_tx, side_rx, tx, rx, grad,
    load_sem, ag_send, ag_mine, ag_other, rs_send, rs_recv, side_send, side_recv,
    store_sem,
):
    n_frames, width = emb.shape
    blocks = n_frames // BLK
    cols = 256
    pieces = n_frames // cols
    temper = 1.0 / math.sqrt(width)

    me = lax.axis_index("vid")
    core = me % 2
    z = (me // 2) % SIDE
    y = me // (2 * SIDE)

    def owner(da, db, other):
        ya = (y + da * (1 - core) + db * core) % SIDE
        zb = (z + db * (1 - core) + da * core) % SIDE
        kind = core + other * (1 - 2 * core)
        return (ya * SIDE + zb) * 2 + kind

    dev = {
        "a+": owner(1, 0, 0), "a-": owner(3, 0, 0),
        "b+": owner(0, 1, 0), "b-": owner(0, 3, 0),
        "side": owner(0, 0, 1),
    }

    load_frames = pltpu.make_async_copy(frames_hbm, frames, load_sem.at[0])
    load_w = pltpu.make_async_copy(w_hbm, w, load_sem.at[1])
    load_frames.start()
    load_w.start()

    barrier = pltpu.get_barrier_semaphore()
    for name in dev:
        pl.semaphore_signal(barrier, inc=1, device_id={"vid": dev[name]}, device_id_type=MESH)
    table[0, 0:BLK, :] = step_in[...]
    pl.semaphore_wait(barrier, len(dev))

    def mine(k):
        return table.at[k, pl.ds(0, BLK)]

    def others(k):
        return table.at[k, pl.ds(BLK, BLK)]

    def remote(src, dst, send, recv, name):
        return pltpu.make_async_remote_copy(
            src_ref=src, dst_ref=dst, send_sem=send, recv_sem=recv,
            device_id={"vid": dev[name]}, device_id_type=MESH,
        )

    sends = []

    def pass_on(place):
        k = POS[place]
        for name in ONWARD.get(place, []):
            sa, sb = SHIFT[name]
            land = POS[((place[0] + sa) % SIDE, (place[1] + sb) % SIDE)]
            sends.append(k)
            remote(mine(k), mine(land), ag_send.at[len(sends) - 1], ag_mine.at[land], name).start()
        sends.append(k)
        remote(
            mine(k), others(TURN[k]), ag_send.at[len(sends) - 1], ag_other.at[TURN[k]], "side"
        ).start()

    def arrive(place):
        k = POS[place]
        remote(mine(k), mine(k), ag_send.at[0], ag_mine.at[k], "side").wait_recv()
        pass_on(place)

    pass_on((0, 0))

    row = lax.broadcasted_iota(jnp.int32, (2 * CHIPS, BLK), 0)
    ids = jnp.zeros((2 * CHIPS, BLK), jnp.int32)
    for k, (da, db) in enumerate(ORDER):
        for other in range(2):
            ids = jnp.where(row == 2 * k + other, owner(da, db, other), ids)
    step_hot = jnp.where(ids == tile_step[...], 1.0, 0.0).astype(BF16)
    block_of = lax.broadcasted_iota(jnp.int32, (n_frames, BLK), 0) // BLK
    slot = lax.broadcasted_iota(jnp.int32, (n_frames, BLK), 1)
    frame_hot = jnp.where(
        (block_of == tile_frame[...]) & (slot < count[0]), 1.0, 0.0
    ).astype(BF16)
    seen = lax.dot_general(step_hot, frame_hot, NT, preferred_element_type=F32)
    hidden = jnp.where(seen > 0.5, 0.0, FAR)
    for k in range(CHIPS):
        bias[k] = hidden[2 * k : 2 * k + 2, :]
    label = lax.broadcasted_iota(jnp.int32, (BLK, BLK), 0)
    for b in range(blocks):
        onehot[:, b * BLK : (b + 1) * BLK] = jnp.where(
            label == tgt[b : b + 1, :], 1.0, 0.0
        ).astype(BF16)
    top[...] = jnp.full_like(top, FAR)
    total[...] = jnp.zeros_like(total)

    load_frames.wait()
    load_w.wait()
    for n in range(pieces):
        rows = slice(n * cols, (n + 1) * cols)
        emb[rows, :] = jnp.dot(
            frames[rows, :], w[...], preferred_element_type=F32
        ).astype(BF16)

    @pl.loop(0, CHIPS)
    def _(k):
        for step in GATHER:
            @pl.when(k == step)
            def _():
                for place in GATHER[step]:
                    arrive(place)
        remote(others(k), others(k), ag_send.at[0], ag_other.at[k], "side").wait_recv()
        tab = table[k]
        for n in range(pieces):
            fs = slice(n * cols, (n + 1) * cols)
            raw = lax.dot_general(tab, emb[fs, :], NT, preferred_element_type=F32)
            low = raw[:BLK] * (temper * LOG2E) + bias[k, 0:1, fs]
            high = raw[BLK:] * (temper * LOG2E) + bias[k, 1:2, fs]
            scores[k, :BLK, fs] = low
            scores[k, BLK:, fs] = high
            peak = jnp.maximum(
                jnp.max(low, axis=0, keepdims=True), jnp.max(high, axis=0, keepdims=True)
            )
            before = top[:, fs]
            after = jnp.maximum(before, peak)
            gained = jnp.sum(jnp.exp2(low - after), axis=0, keepdims=True) + jnp.sum(
                jnp.exp2(high - after), axis=0, keepdims=True
            )
            total[:, fs] = total[:, fs] * jnp.exp2(before - after) + gained
            top[:, fs] = after
        table_t[:, pl.ds(pl.multiple_of(k * 2 * BLK, 2 * BLK), 2 * BLK)] = tab.T

    shift[...] = top[...] + jnp.log(total[...]) * LOG2E
    for b in range(blocks):
        fs = slice(b * BLK, (b + 1) * BLK)
        kept = jnp.where(label == tgt[b : b + 1, :], scores[0, 0:BLK, fs], 0.0)
        positive = jnp.sum(kept, axis=0, keepdims=True)
        loss[b : b + 1, :] = (shift[:, fs] - positive) * LN2

    def landed(name):
        i = LAND[name]
        remote(rx.at[i], rx.at[i], ag_send.at[0], rs_recv.at[i], "side").wait_recv()
        return rx[i].astype(F32)

    def gathered(place):
        k = POS[place]
        remote(side_rx.at[k], side_rx.at[k], ag_send.at[0], side_recv.at[k], "side").wait_recv()
        return part[k] + side_rx[k].astype(F32)

    def combine(place):
        takes, name, land = COMBINE[place]
        value = gathered(place)
        for take in takes:
            value = value + landed(take)
        i = LAND[land]
        tx[i] = value.astype(BF16)
        remote(tx.at[i], rx.at[i], rs_send.at[i], rs_recv.at[i], name).start()

    def to_side(k):
        return remote(
            side_tx.at[k], side_rx.at[TURN[k]], side_send.at[k], side_recv.at[TURN[k]], "side"
        )

    @pl.loop(0, CHIPS)
    def _(i):
        k = CHIPS - 1 - i
        base = pl.multiple_of(k * 2 * BLK, 2 * BLK)
        for n in range(pieces):
            fs = slice(n * cols, (n + 1) * cols)
            probs[pl.ds(base, 2 * BLK), fs] = jnp.exp2(scores[k, :, fs] - shift[:, fs]).astype(BF16)
        out = jnp.dot(probs[pl.ds(base, 2 * BLK), :], emb[...], preferred_element_type=F32)
        part[k] = out[:BLK]
        side_tx[k] = out[BLK:].astype(BF16)
        for step in range(CHIPS):
            @pl.when(i == step)
            def _():
                to_side(CHIPS - 1 - step).start()
                for place in REDUCE.get(step, []):
                    combine(place)

    own[...] = jnp.dot(onehot[...], emb[...], preferred_element_type=F32)

    @pl.loop(0, pieces)
    def _(n):
        fs = pl.ds(pl.multiple_of(n * cols, cols), cols)
        toward = jnp.dot(table_t[...], probs[:, fs], preferred_element_type=F32)
        chosen = jnp.dot(table_t[:, 0:BLK], onehot[:, fs], preferred_element_type=F32)
        rows = ((toward - chosen) * temper).astype(BF16).T
        grad[fs, :] = lax.dot_general(rows, w[...], NT, preferred_element_type=F32).astype(BF16)
        pltpu.make_async_copy(grad.at[fs], grad_hbm.at[fs], store_sem.at[n]).start()

    value = gathered((0, 0)) - own[...]
    for take in ["p0", "m0", "Am", "Ap"]:
        value = value + landed(take)
    step_grad[...] = value * temper

    for n in range(pieces):
        fs = pl.ds(n * cols, cols)
        pltpu.make_async_copy(grad.at[fs], grad_hbm.at[fs], store_sem.at[n]).wait()
    for i, k in enumerate(sends):
        remote(mine(k), mine(k), ag_send.at[i], ag_mine.at[k], "side").wait_send()
    for i in range(len(LANDS)):
        remote(tx.at[i], rx.at[i], rs_send.at[i], rs_recv.at[i], "side").wait_send()
    for k in range(CHIPS):
        to_side(k).wait_send()


def shards(frames, w_frame, step_emb, targets, tile_frame, tile_step, tile_count):
    n_frames, depth = frames.shape
    steps, width = step_emb.shape
    blocks = n_frames // BLK
    vmem = pl.BlockSpec(memory_space=pltpu.VMEM)
    anywhere = pl.BlockSpec(memory_space=pl.ANY)
    dma = pltpu.SemaphoreType.DMA
    pieces = n_frames // 256
    loss, grad, step_grad = pl.pallas_call(
        kernel,
        name="contrastive",
        out_shape=(
            jax.ShapeDtypeStruct((blocks, BLK), F32),
            jax.ShapeDtypeStruct((n_frames, depth), BF16),
            jax.ShapeDtypeStruct((steps, width), F32),
        ),
        in_specs=[vmem, vmem, vmem, vmem, pl.BlockSpec(memory_space=pltpu.SMEM), anywhere, anywhere],
        out_specs=(vmem, anywhere, vmem),
        scratch_shapes=[
            pltpu.VMEM((n_frames, depth), BF16),
            pltpu.VMEM((depth, width), BF16),
            pltpu.VMEM((n_frames, width), BF16),
            pltpu.VMEM((CHIPS, 2 * BLK, width), BF16),
            pltpu.VMEM((width, CHIPS * 2 * BLK), BF16),
            pltpu.VMEM((CHIPS, 2 * BLK, n_frames), F32),
            pltpu.VMEM((CHIPS * 2 * BLK, n_frames), BF16),
            pltpu.VMEM((CHIPS, 2, n_frames), F32),
            pltpu.VMEM((1, n_frames), F32),
            pltpu.VMEM((1, n_frames), F32),
            pltpu.VMEM((1, n_frames), F32),
            pltpu.VMEM((BLK, n_frames), BF16),
            pltpu.VMEM((BLK, width), F32),
            pltpu.VMEM((CHIPS, BLK, width), F32),
            pltpu.VMEM((CHIPS, BLK, width), BF16),
            pltpu.VMEM((CHIPS, BLK, width), BF16),
            pltpu.VMEM((len(LANDS), BLK, width), BF16),
            pltpu.VMEM((len(LANDS), BLK, width), BF16),
            pltpu.VMEM((n_frames, depth), BF16),
            dma((2,)),
            dma((31,)),
            dma((CHIPS,)),
            dma((CHIPS,)),
            dma((len(LANDS),)),
            dma((len(LANDS),)),
            dma((CHIPS,)),
            dma((CHIPS,)),
            dma((pieces,)),
        ],
        compiler_params=pltpu.CompilerParams(
            collective_id=0, has_side_effects=True, vmem_limit_bytes=60 * 1024 * 1024
        ),
    )(
        step_emb, targets.reshape(blocks, BLK), tile_frame, tile_step, tile_count, frames, w_frame,
    )
    return (loss.reshape(n_frames), grad, step_grad)


def solution(mesh):
    placed = (
        P(("grp", "vid"), None),
        P(),
        P(("grp", "vid"), None),
        P(("grp", "vid")),
        P(("grp", "vid"), None),
        P(("grp", "vid"), None),
        P(("grp", "vid")),
    )
    return jax.shard_map(
        shards,
        mesh=mesh,
        in_specs=placed,
        out_specs=(P(("grp", "vid")), P(("grp", "vid"), None), P(("grp", "vid"), None)),
        check_vma=False,
    )
```

```python
import functools
import math

import jax
import jax.numpy as jnp
from jax import lax
from jax.experimental import pallas as pl
from jax.experimental.pallas import tpu as pltpu
from jax.sharding import PartitionSpec as P

F32 = jnp.float32
BF16 = jnp.bfloat16
MESH = pl.DeviceIdType.MESH
NT = (((1,), (1,)), ((), ()))
SIDE = 4
CHIPS = SIDE * SIDE
BLK = 128
LOG2E = 1.0 / math.log(2.0)
LN2 = math.log(2.0)
FAR = -1e30

ORDER = [
    (0, 0), (0, 1), (1, 0), (0, 3), (3, 0), (1, 1), (3, 3), (1, 3),
    (3, 1), (2, 0), (0, 2), (2, 1), (1, 2), (2, 3), (3, 2), (2, 2),
]
POS = {place: k for k, place in enumerate(ORDER)}
TURN = [POS[(db, da)] for da, db in ORDER]

GATHER = {
    0: [(3, 0), (1, 0), (2, 0), (0, 3), (0, 1)],
    3: [(3, 3), (3, 1)],
    4: [(1, 1), (1, 3)],
    5: [(2, 1), (2, 3)],
    7: [(0, 2)],
    8: [(3, 2), (1, 2)],
    11: [(2, 2)],
}
ONWARD = {
    (0, 0): ["a2", "a+", "a-", "b+", "b-"],
    (3, 0): ["b+", "b-"],
    (1, 0): ["b+", "b-"],
    (2, 0): ["b+", "b-"],
    (0, 3): ["b+"],
    (1, 3): ["b+"],
    (2, 1): ["b-"],
    (3, 1): ["b-"],
}
SHIFT = {"a+": (-1, 0), "a-": (1, 0), "a2": (-2, 0), "b+": (0, -1), "b-": (0, 1)}

LANDS = ["h0", "h1", "h2", "h3", "p0", "p1", "p2", "p3",
         "m0", "m1", "m2", "m3", "A2", "Ap", "Am"]
LAND = {name: i for i, name in enumerate(LANDS)}
COMBINE = {
    (2, 2): ([], "b-", "h2"),
    (3, 2): ([], "b-", "h3"),
    (1, 2): ([], "b+", "h1"),
    (0, 2): ([], "b+", "h0"),
    (2, 3): (["h2"], "b-", "m2"),
    (3, 3): (["h3"], "b-", "m3"),
    (1, 3): ([], "b-", "m1"),
    (0, 3): ([], "b-", "m0"),
    (2, 1): ([], "b+", "p2"),
    (3, 1): ([], "b+", "p3"),
    (1, 1): (["h1"], "b+", "p1"),
    (0, 1): (["h0"], "b+", "p0"),
    (2, 0): (["p2", "m2"], "a2", "A2"),
    (1, 0): (["p1", "m1"], "a+", "Ap"),
    (3, 0): (["p3", "m3"], "a-", "Am"),
}
REDUCE = {
    4: [(2, 2)],
    6: [(3, 2)],
    8: [(2, 1), (1, 2)],
    10: [(0, 2)],
    12: [(3, 1), (1, 3), (2, 3)],
    13: [(3, 3)],
    14: [(1, 1)],
}
REDUCE_LATE = {
    (0, 0): [(0, 3)],
    (0, 1): [(0, 1)],
    (1, 0): [(2, 0)],
    (1, 1): [(3, 0), (1, 0)],
}
EARLY = 8
LATE = CHIPS - EARLY


def kernel(
    step_in, tgt, tile_frame, tile_step, count, frames_hbm, w_hbm,
    loss, grad, step_grad,
    frames, w, emb, table, table_t, step_t, scores, probs, near, toward, bias, top, total,
    shift, onehot, own, turned_rows, part, side_tx, side_rx, tx, rx,
    load_sem, ag_send, ag_mine, ag_other, rs_send, rs_recv, side_send, side_recv,
):
    n_frames, width = emb.shape
    blocks = n_frames // BLK
    cols = 256
    pieces = n_frames // cols
    temper = 1.0 / math.sqrt(width)

    me = lax.axis_index("vid")
    core = me % 2
    z = (me // 2) % SIDE
    y = me // (2 * SIDE)

    def owner(da, db, other):
        ya = (y + da * (1 - core) + db * core) % SIDE
        zb = (z + db * (1 - core) + da * core) % SIDE
        kind = core + other * (1 - 2 * core)
        return (ya * SIDE + zb) * 2 + kind

    dev = {
        "a+": owner(1, 0, 0), "a-": owner(3, 0, 0), "a2": owner(2, 0, 0),
        "b+": owner(0, 1, 0), "b-": owner(0, 3, 0),
        "side": owner(0, 0, 1),
    }

    load_frames = pltpu.make_async_copy(frames_hbm, frames, load_sem.at[0])
    load_w = pltpu.make_async_copy(w_hbm, w, load_sem.at[1])
    load_frames.start()
    load_w.start()

    barrier = pltpu.get_barrier_semaphore()
    for name in dev:
        pl.semaphore_signal(barrier, inc=1, device_id={"vid": dev[name]}, device_id_type=MESH)
    table[0, 0:BLK, :] = step_in[...]
    row = lax.broadcasted_iota(jnp.int32, (2 * CHIPS, BLK), 0)
    ids = jnp.zeros((2 * CHIPS, BLK), jnp.int32)
    for k, (da, db) in enumerate(ORDER):
        for other in range(2):
            ids = jnp.where(row == 2 * k + other, owner(da, db, other), ids)
    step_hot = jnp.where(ids == tile_step[...], 1.0, 0.0).astype(BF16)
    block_of = lax.broadcasted_iota(jnp.int32, (n_frames, BLK), 0) // BLK
    slot = lax.broadcasted_iota(jnp.int32, (n_frames, BLK), 1)
    frame_hot = jnp.where(
        (block_of == tile_frame[...]) & (slot < count[...]), 1.0, 0.0
    ).astype(BF16)
    seen = lax.dot_general(step_hot, frame_hot, NT, preferred_element_type=F32)
    hidden = jnp.where(seen > 0.5, 0.0, FAR)
    for k in range(CHIPS):
        bias[k] = hidden[2 * k : 2 * k + 2, :]
    label = lax.broadcasted_iota(jnp.int32, (BLK, BLK), 0)
    for b in range(blocks):
        onehot[:, b * BLK : (b + 1) * BLK] = jnp.where(
            label == tgt[b : b + 1, :], 1.0, 0.0
        ).astype(BF16)
    top[...] = jnp.full_like(top, FAR)
    total[...] = jnp.zeros_like(total)

    toward[...] = jnp.zeros_like(toward)
    step_t[...] = step_in[...].T
    pl.semaphore_wait(barrier, len(dev))

    def mine(k):
        return table.at[k, pl.ds(0, BLK)]

    def others(k):
        return table.at[k, pl.ds(BLK, BLK)]

    def remote(src, dst, send, recv, name):
        return pltpu.make_async_remote_copy(
            src_ref=src, dst_ref=dst, send_sem=send, recv_sem=recv,
            device_id={"vid": dev[name]}, device_id_type=MESH,
        )

    sends = []

    def pass_on(place):
        k = POS[place]
        for name in ONWARD.get(place, []):
            sa, sb = SHIFT[name]
            land = POS[((place[0] + sa) % SIDE, (place[1] + sb) % SIDE)]
            sends.append(k)
            remote(mine(k), mine(land), ag_send.at[len(sends) - 1], ag_mine.at[land], name).start()
        sends.append(k)
        remote(
            mine(k), others(TURN[k]), ag_send.at[len(sends) - 1], ag_other.at[TURN[k]], "side"
        ).start()

    def arrive(place):
        k = POS[place]
        remote(mine(k), mine(k), ag_send.at[0], ag_mine.at[k], "side").wait_recv()
        pass_on(place)

    pass_on((0, 0))

    load_frames.wait()
    load_w.wait()
    for n in range(pieces):
        rows = slice(n * cols, (n + 1) * cols)
        emb[rows, :] = jnp.dot(
            frames[rows, :], w[...], preferred_element_type=F32
        ).astype(BF16)

    def score(k, early):
        for step in GATHER:
            if (step < EARLY) == early:
                @pl.when(k == step)
                def _():
                    for place in GATHER[step]:
                        arrive(place)
        remote(others(k), others(k), ag_send.at[0], ag_other.at[k], "side").wait_recv()
        tab = table[k]
        turned = tab.T
        if not early:
            base = pl.multiple_of((k - EARLY) * 2 * BLK, 2 * BLK)
            table_t[:, pl.ds(base, 2 * BLK)] = turned
        for n in range(pieces):
            fs = slice(n * cols, (n + 1) * cols)
            raw = lax.dot_general(tab, emb[fs, :], NT, preferred_element_type=F32)
            low = raw[:BLK] * (temper * LOG2E) + bias[k, 0:1, fs]
            high = raw[BLK:] * (temper * LOG2E) + bias[k, 1:2, fs]
            scores[k, :BLK, fs] = low
            scores[k, BLK:, fs] = high
            peak = jnp.maximum(
                jnp.max(low, axis=0, keepdims=True), jnp.max(high, axis=0, keepdims=True)
            )
            before = top[:, fs]
            after = jnp.maximum(before, peak)
            fade = jnp.exp2(before - after)
            low = jnp.exp2(low - after)
            high = jnp.exp2(high - after)
            gained = jnp.sum(low, axis=0, keepdims=True) + jnp.sum(high, axis=0, keepdims=True)
            total[:, fs] = total[:, fs] * fade + gained
            top[:, fs] = after
            if early:
                near[:BLK, fs] = low.astype(BF16)
                near[BLK:, fs] = high.astype(BF16)
                toward[:, fs] = toward[:, fs] * fade + jnp.dot(
                    turned, near[:, fs], preferred_element_type=F32
                )

    @pl.loop(0, EARLY)
    def _(k):
        score(k, True)

    shift[...] = top[...]

    @pl.loop(EARLY, CHIPS)
    def _(k):
        score(k, False)

    lse = top[...] + jnp.log(total[...]) * LOG2E
    top[...] = jnp.exp2(shift[...] - lse)
    shift[...] = lse
    for b in range(blocks):
        fs = slice(b * BLK, (b + 1) * BLK)
        kept = jnp.where(label == tgt[b : b + 1, :], scores[0, 0:BLK, fs], 0.0)
        positive = jnp.sum(kept, axis=0, keepdims=True)
        loss[b : b + 1, :] = (shift[:, fs] - positive) * LN2

    def landed(name):
        i = LAND[name]
        remote(rx.at[i], rx.at[i], ag_send.at[0], rs_recv.at[i], "side").wait_recv()
        return rx[i].astype(F32)

    def gathered(place):
        k = POS[place]
        remote(side_rx.at[k], side_rx.at[k], ag_send.at[0], side_recv.at[k], "side").wait_recv()
        return part[k] + side_rx[k].astype(F32)

    def combine(place):
        takes, name, land = COMBINE[place]
        value = gathered(place)
        for take in takes:
            value = value + landed(take)
        i = LAND[land]
        tx[i] = value.astype(BF16)
        remote(tx.at[i], rx.at[i], rs_send.at[i], rs_recv.at[i], name).start()

    def to_side(k):
        return remote(
            side_tx.at[k], side_rx.at[TURN[k]], side_send.at[k], side_recv.at[TURN[k]], "side"
        )

    @pl.loop(0, CHIPS)
    def _(i):
        k = CHIPS - 1 - i
        base = pl.multiple_of(k * 2 * BLK, 2 * BLK)
        for n in range(pieces):
            fs = slice(n * cols, (n + 1) * cols)
            probs[pl.ds(base, 2 * BLK), fs] = jnp.exp2(scores[k, :, fs] - shift[:, fs]).astype(BF16)
        out = jnp.dot(probs[pl.ds(base, 2 * BLK), :], emb[...], preferred_element_type=F32)
        part[k] = out[:BLK]
        side_tx[k] = out[BLK:].astype(BF16)
        for step in range(CHIPS):
            @pl.when(i == step)
            def _():
                to_side(CHIPS - 1 - step).start()
                for place in REDUCE.get(step, []):
                    combine(place)

    own[...] = jnp.dot(onehot[...], emb[...], preferred_element_type=F32)

    @pl.loop(0, pieces)
    def _(n):
        for (piece, half), places in REDUCE_LATE.items():
            if half == 0:
                @pl.when(n == piece)
                def _():
                    for place in places:
                        combine(place)
        fs = pl.ds(pl.multiple_of(n * cols, cols), cols)
        rows = toward[:, fs] * top[:, fs] - jnp.dot(
            step_t[...], onehot[:, fs], preferred_element_type=F32
        )
        rows = rows + jnp.dot(
            table_t[...], probs[EARLY * 2 * BLK :, fs], preferred_element_type=F32
        )
        rows_t = (rows * temper).astype(BF16).T
        turned_rows[...] = rows_t
        for (piece, half), places in REDUCE_LATE.items():
            if half == 1:
                @pl.when(n == piece)
                def _():
                    for place in places:
                        combine(place)
        grad[fs, :] = lax.dot_general(
            turned_rows[...], w[...], NT, preferred_element_type=F32
        ).astype(BF16)

    value = gathered((0, 0)) - own[...]
    for take in ["p0", "m0", "Am", "A2", "Ap"]:
        value = value + landed(take)
    step_grad[...] = value * temper

    for i, k in enumerate(sends):
        remote(mine(k), mine(k), ag_send.at[i], ag_mine.at[k], "side").wait_send()
    for i in range(len(LANDS)):
        remote(tx.at[i], rx.at[i], rs_send.at[i], rs_recv.at[i], "side").wait_send()
    for k in range(CHIPS):
        to_side(k).wait_send()


def hand_over(loss, grad, step_grad, loss_out, grad_out, step_grad_out, sem):
    copies = [
        pltpu.make_async_copy(grad, grad_out, sem.at[0]),
        pltpu.make_async_copy(step_grad, step_grad_out, sem.at[1]),
        pltpu.make_async_copy(loss, loss_out, sem.at[2]),
    ]
    for copy in copies:
        copy.start()
    for copy in copies:
        copy.wait()


def shards(frames, w_frame, step_emb, targets, tile_frame, tile_step, tile_count):
    n_frames, depth = frames.shape
    steps, width = step_emb.shape
    blocks = n_frames // BLK
    vmem = pl.BlockSpec(memory_space=pltpu.VMEM)
    anywhere = pl.BlockSpec(memory_space=pl.ANY)
    dma = pltpu.SemaphoreType.DMA
    results = (
        jax.ShapeDtypeStruct((blocks, BLK), F32),
        jax.ShapeDtypeStruct((n_frames, depth), BF16),
        jax.ShapeDtypeStruct((steps, width), F32),
    )
    held = tuple(pltpu.VMEM(r.shape, r.dtype) for r in results)
    found = pl.pallas_call(
        kernel,
        name="contrastive",
        out_shape=held,
        in_specs=[vmem] * 5 + [anywhere] * 2,
        out_specs=(vmem,) * 3,
        scratch_shapes=[
            pltpu.VMEM((n_frames, depth), BF16),
            pltpu.VMEM((depth, width), BF16),
            pltpu.VMEM((n_frames, width), BF16),
            pltpu.VMEM((CHIPS, 2 * BLK, width), BF16),
            pltpu.VMEM((width, LATE * 2 * BLK), BF16),
            pltpu.VMEM((width, BLK), BF16),
            pltpu.VMEM((CHIPS, 2 * BLK, n_frames), F32),
            pltpu.VMEM((CHIPS * 2 * BLK, n_frames), BF16),
            pltpu.VMEM((2 * BLK, n_frames), BF16),
            pltpu.VMEM((width, n_frames), F32),
            pltpu.VMEM((CHIPS, 2, n_frames), F32),
            pltpu.VMEM((1, n_frames), F32),
            pltpu.VMEM((1, n_frames), F32),
            pltpu.VMEM((1, n_frames), F32),
            pltpu.VMEM((BLK, n_frames), BF16),
            pltpu.VMEM((BLK, width), F32),
            pltpu.VMEM((2 * BLK, width), BF16),
            pltpu.VMEM((CHIPS, BLK, width), F32),
            pltpu.VMEM((CHIPS, BLK, width), BF16),
            pltpu.VMEM((CHIPS, BLK, width), BF16),
            pltpu.VMEM((len(LANDS), BLK, width), BF16),
            pltpu.VMEM((len(LANDS), BLK, width), BF16),
            dma((2,)),
            dma((31,)),
            dma((CHIPS,)),
            dma((CHIPS,)),
            dma((len(LANDS),)),
            dma((len(LANDS),)),
            dma((CHIPS,)),
            dma((CHIPS,)),
        ],
        compiler_params=pltpu.CompilerParams(
            collective_id=0, has_side_effects=True, vmem_limit_bytes=54 * 1024 * 1024
        ),
    )(
        step_emb, targets.reshape(blocks, BLK), tile_frame, tile_step,
        tile_count.reshape(1, 1), frames, w_frame,
    )
    loss, grad, step_grad = pl.pallas_call(
        hand_over,
        name="hand_over",
        out_shape=results,
        in_specs=[pl.BlockSpec(memory_space=pltpu.VMEM)] * 3,
        out_specs=(anywhere,) * 3,
        scratch_shapes=[dma((3,))],
    )(*[pltpu.with_memory_space_constraint(f, pltpu.VMEM) for f in found])
    return (loss.reshape(n_frames), grad, step_grad)


def solution(mesh):
    placed = (
        P(("grp", "vid"), None),
        P(),
        P(("grp", "vid"), None),
        P(("grp", "vid")),
        P(("grp", "vid"), None),
        P(("grp", "vid"), None),
        P(("grp", "vid")),
    )
    return jax.shard_map(
        shards,
        mesh=mesh,
        in_specs=placed,
        out_specs=(P(("grp", "vid")), P(("grp", "vid"), None), P(("grp", "vid"), None)),
        check_vma=False,
    )
```

```python
import functools
import math

import jax
import jax.numpy as jnp
from jax import lax
from jax.experimental import pallas as pl
from jax.experimental.pallas import tpu as pltpu
from jax.sharding import PartitionSpec as P

F32 = jnp.float32
BF16 = jnp.bfloat16
MESH = pl.DeviceIdType.MESH
NT = (((1,), (1,)), ((), ()))
SIDE = 4
CHIPS = SIDE * SIDE
BLK = 128
LOG2E = 1.0 / math.log(2.0)
LN2 = math.log(2.0)
FAR = -1e30

ORDER = [
    (0, 0), (0, 1), (1, 0), (0, 3), (3, 0), (1, 1), (3, 3), (1, 3),
    (3, 1), (2, 0), (0, 2), (2, 1), (1, 2), (2, 3), (3, 2), (2, 2),
]
POS = {place: k for k, place in enumerate(ORDER)}
TURN = [POS[(db, da)] for da, db in ORDER]

GATHER = {1: [(3, 0), (1, 0), (2, 0), (0, 3), (0, 1)], 3: [(3, 3), (3, 1)], 4: [(1, 1), (1, 3)], 5: [(2, 1), (2, 3)], 7: [(0, 2)], 8: [(3, 2), (1, 2)], 11: [(2, 2)]}
ONWARD = {
    (0, 0): ["a2", "a+", "a-", "b+", "b-"],
    (3, 0): ["b+", "b-"],
    (1, 0): ["b+", "b-"],
    (2, 0): ["b+", "b-"],
    (0, 3): ["b+"],
    (1, 3): ["b+"],
    (2, 1): ["b-"],
    (3, 1): ["b-"],
}
SHIFT = {"a+": (-1, 0), "a-": (1, 0), "a2": (-2, 0), "b+": (0, -1), "b-": (0, 1), "b2": (0, -2)}

LANDS = ["h0", "h1", "h2", "h3", "p0", "p1", "p2", "p3",
         "m0", "m1", "m2", "m3", "A2", "Ap", "Am"]
LAND = {name: i for i, name in enumerate(LANDS)}
COMBINE = {
    (2, 2): ([], "b-", "h2"),
    (3, 2): ([], "b-", "h3"),
    (1, 2): ([], "b+", "h1"),
    (0, 2): ([], "b+", "h0"),
    (2, 3): (["h2"], "b-", "m2"),
    (3, 3): (["h3"], "b-", "m3"),
    (1, 3): ([], "b-", "m1"),
    (0, 3): ([], "b-", "m0"),
    (2, 1): ([], "b+", "p2"),
    (3, 1): ([], "b+", "p3"),
    (1, 1): (["h1"], "b+", "p1"),
    (0, 1): (["h0"], "b+", "p0"),
    (2, 0): (["p2", "m2"], "a2", "A2"),
    (1, 0): (["p1", "m1"], "a+", "Ap"),
    (3, 0): (["p3", "m3"], "a-", "Am"),
}
REDUCE = {
    4: [(2, 2)],
    6: [(3, 2)],
    8: [(2, 1), (1, 2)],
    10: [(0, 2)],
    12: [(3, 1), (1, 3), (2, 3)],
    13: [(3, 3)],
    14: [(1, 1)],
}
REDUCE_LATE = {
    (0, 0): [(0, 3)],
    (0, 1): [(0, 1)],
    (1, 0): [(2, 0)],
    (1, 1): [(3, 0), (1, 0)],
}
EARLY = 4
LATE = CHIPS - EARLY
GROUP = 1


def kernel(
    step_hbm, tgt_hbm, tile_frame_hbm, tile_step_hbm, count_hbm, frames_hbm, w_hbm,
    loss, grad, step_grad,
    frames, w, emb, table, table_t, step_t, scores, probs, near, toward, bias, top, total,
    shift, onehot, own, turned_rows, part, side_tx, side_rx, tx, rx, emb_t,
    tgt, tile_frame, tile_step, count,
    load_sem, ag_send, ag_mine, ag_other, rs_send, rs_recv, side_send, side_recv,
):
    n_frames, width = emb.shape
    blocks = n_frames // BLK
    cols = 256
    pieces = n_frames // cols
    temper = 1.0 / math.sqrt(width)

    me = lax.axis_index("vid")
    core = me % 2
    z = (me // 2) % SIDE
    y = me // (2 * SIDE)

    def owner(da, db, other):
        ya = (y + da * (1 - core) + db * core) % SIDE
        zb = (z + db * (1 - core) + da * core) % SIDE
        kind = core + other * (1 - 2 * core)
        return (ya * SIDE + zb) * 2 + kind

    dev = {
        "a+": owner(1, 0, 0), "a-": owner(3, 0, 0), "a2": owner(2, 0, 0),
        "b+": owner(0, 1, 0), "b-": owner(0, 3, 0), "b2": owner(0, 2, 0),
        "side": owner(0, 0, 1),
    }

    barrier = pltpu.get_barrier_semaphore()
    for name in dev:
        pl.semaphore_signal(barrier, inc=1, device_id={"vid": dev[name]}, device_id_type=MESH)
    loads = [
        pltpu.make_async_copy(src, dst, load_sem.at[i])
        for i, (src, dst) in enumerate([
            (tile_frame_hbm, tile_frame), (tile_step_hbm, tile_step), (count_hbm, count),
            (tgt_hbm, tgt), (step_hbm, table.at[0, pl.ds(0, BLK)]),
            (frames_hbm, frames), (w_hbm, w),
        ])
    ]
    for load in loads:
        load.start()
    toward[...] = jnp.zeros_like(toward)
    for load in loads[:5]:
        load.wait()

    row = lax.broadcasted_iota(jnp.int32, (2 * CHIPS, BLK), 0)
    ids = jnp.zeros((2 * CHIPS, BLK), jnp.int32)
    for k, (da, db) in enumerate(ORDER):
        for other in range(2):
            ids = jnp.where(row == 2 * k + other, owner(da, db, other), ids)
    step_hot = jnp.where(ids == tile_step[...], 1.0, 0.0).astype(BF16)
    block_of = lax.broadcasted_iota(jnp.int32, (n_frames, BLK), 0) // BLK
    slot = lax.broadcasted_iota(jnp.int32, (n_frames, BLK), 1)
    frame_hot = jnp.where(
        (block_of == tile_frame[...]) & (slot < count[...]), 1.0, 0.0
    ).astype(BF16)
    seen = lax.dot_general(step_hot, frame_hot, NT, preferred_element_type=F32)
    hidden = jnp.where(seen > 0.5, 0.0, FAR)
    for k in range(CHIPS):
        bias[k] = hidden[2 * k : 2 * k + 2, :]
    label = lax.broadcasted_iota(jnp.int32, (BLK, BLK), 0)
    for b in range(blocks):
        onehot[:, b * BLK : (b + 1) * BLK] = jnp.where(
            label == tgt[b : b + 1, :], 1.0, 0.0
        ).astype(BF16)
    top[...] = jnp.full_like(top, FAR)
    total[...] = jnp.zeros_like(total)

    step_t[...] = table[0, 0:BLK, :].T
    pl.semaphore_wait(barrier, len(dev))

    def mine(k):
        return table.at[k, pl.ds(0, BLK)]

    def others(k):
        return table.at[k, pl.ds(BLK, BLK)]

    def remote(src, dst, send, recv, name):
        return pltpu.make_async_remote_copy(
            src_ref=src, dst_ref=dst, send_sem=send, recv_sem=recv,
            device_id={"vid": dev[name]}, device_id_type=MESH,
        )

    sends = []

    def pass_on(place):
        k = POS[place]
        for name in ONWARD.get(place, []):
            sa, sb = SHIFT[name]
            land = POS[((place[0] + sa) % SIDE, (place[1] + sb) % SIDE)]
            sends.append(k)
            remote(mine(k), mine(land), ag_send.at[len(sends) - 1], ag_mine.at[land], name).start()
        sends.append(k)
        remote(
            mine(k), others(TURN[k]), ag_send.at[len(sends) - 1], ag_other.at[TURN[k]], "side"
        ).start()

    def arrive(place):
        k = POS[place]
        remote(mine(k), mine(k), ag_send.at[0], ag_mine.at[k], "side").wait_recv()
        pass_on(place)

    pass_on((0, 0))

    for load in loads[5:]:
        load.wait()
    for n in range(pieces):
        rows = slice(n * cols, (n + 1) * cols)
        emb[rows, :] = jnp.dot(
            frames[rows, :], w[...], preferred_element_type=F32
        ).astype(BF16)
        emb_t[:, rows] = emb[rows, :].T

    def score(k, early):
        for step in GATHER:
            if (step * GROUP < EARLY) == early:
                @pl.when(k == step)
                def _():
                    for place in GATHER[step]:
                        arrive(place)
        tabs, turns = [], []
        for g in range(GROUP):
            j = k * GROUP + g
            remote(others(j), others(j), ag_send.at[0], ag_other.at[j], "side").wait_recv()
            tabs.append(table[j])
            turns.append(tabs[-1].T)
        tab = jnp.concatenate(tabs, axis=0)
        turned = jnp.concatenate(turns, axis=1)
        tall = 2 * BLK * GROUP
        if not early:
            base = pl.multiple_of((k * GROUP - EARLY) * 2 * BLK, tall)
            table_t[:, pl.ds(base, tall)] = turned
        for n in range(pieces):
            fs = slice(n * cols, (n + 1) * cols)
            raw = jnp.dot(tab, emb_t[:, fs], preferred_element_type=F32)
            parts = []
            before = top[:, fs]
            after = before
            for g in range(2 * GROUP):
                j, h = g // 2, g % 2
                value = raw[g * BLK : (g + 1) * BLK] * (temper * LOG2E) + bias[
                    k * GROUP + j, h : h + 1, fs
                ]
                scores[k * GROUP + j, h * BLK : (h + 1) * BLK, fs] = value
                after = jnp.maximum(after, jnp.max(value, axis=0, keepdims=True))
                parts.append(value)
            fade = jnp.exp2(before - after)
            gained = total[:, fs] * fade
            for g in range(2 * GROUP):
                value = jnp.exp2(parts[g] - after)
                gained = gained + jnp.sum(value, axis=0, keepdims=True)
                if early:
                    near[g * BLK : (g + 1) * BLK, fs] = value.astype(BF16)
            total[:, fs] = gained
            top[:, fs] = after
            if early:
                toward[:, fs] = toward[:, fs] * fade + jnp.dot(
                    turned, near[:, fs], preferred_element_type=F32
                )

    @pl.loop(0, EARLY // GROUP)
    def _(k):
        score(k, True)

    shift[...] = top[...]

    @pl.loop(EARLY // GROUP, CHIPS // GROUP)
    def _(k):
        score(k, False)

    lse = top[...] + jnp.log(total[...]) * LOG2E
    top[...] = jnp.exp2(shift[...] - lse)
    shift[...] = lse
    for b in range(blocks):
        fs = slice(b * BLK, (b + 1) * BLK)
        kept = jnp.where(label == tgt[b : b + 1, :], scores[0, 0:BLK, fs], 0.0)
        positive = jnp.sum(kept, axis=0, keepdims=True)
        loss[b : b + 1, :] = (shift[:, fs] - positive) * LN2

    def landed(name):
        i = LAND[name]
        remote(rx.at[i], rx.at[i], ag_send.at[0], rs_recv.at[i], "side").wait_recv()
        return rx[i].astype(F32)

    def gathered(place):
        k = POS[place]
        remote(side_rx.at[k], side_rx.at[k], ag_send.at[0], side_recv.at[k], "side").wait_recv()
        return part[k] + side_rx[k].astype(F32)

    def combine(place):
        takes, name, land = COMBINE[place]
        value = gathered(place)
        for take in takes:
            value = value + landed(take)
        i = LAND[land]
        tx[i] = value.astype(BF16)
        remote(tx.at[i], rx.at[i], rs_send.at[i], rs_recv.at[i], name).start()

    def to_side(k):
        return remote(
            side_tx.at[k], side_rx.at[TURN[k]], side_send.at[k], side_recv.at[TURN[k]], "side"
        )

    @pl.loop(0, CHIPS)
    def _(i):
        k = CHIPS - 1 - i
        base = pl.multiple_of(k * 2 * BLK, 2 * BLK)
        for n in range(pieces):
            fs = slice(n * cols, (n + 1) * cols)
            probs[pl.ds(base, 2 * BLK), fs] = jnp.exp2(scores[k, :, fs] - shift[:, fs]).astype(BF16)
        out = jnp.dot(probs[pl.ds(base, 2 * BLK), :], emb[...], preferred_element_type=F32)
        part[k] = out[:BLK]
        side_tx[k] = out[BLK:].astype(BF16)
        for step in range(CHIPS):
            @pl.when(i == step)
            def _():
                to_side(CHIPS - 1 - step).start()
                for place in REDUCE.get(step, []):
                    combine(place)

    own[...] = jnp.dot(onehot[...], emb[...], preferred_element_type=F32)

    @pl.loop(0, pieces)
    def _(n):
        for (piece, half), places in REDUCE_LATE.items():
            if half == 0:
                @pl.when(n == piece)
                def _():
                    for place in places:
                        combine(place)
        fs = pl.ds(pl.multiple_of(n * cols, cols), cols)
        rows = toward[:, fs] * top[:, fs] - jnp.dot(
            step_t[...], onehot[:, fs], preferred_element_type=F32
        )
        rows = rows + jnp.dot(
            table_t[...], probs[EARLY * 2 * BLK :, fs], preferred_element_type=F32
        )
        rows_t = (rows * temper).astype(BF16).T
        turned_rows[...] = rows_t
        for (piece, half), places in REDUCE_LATE.items():
            if half == 1:
                @pl.when(n == piece)
                def _():
                    for place in places:
                        combine(place)
        grad[fs, :] = lax.dot_general(
            turned_rows[...], w[...], NT, preferred_element_type=F32
        ).astype(BF16)

    value = gathered((0, 0)) - own[...]
    for take in ["p0", "m0", "Am", "A2", "Ap"]:
        value = value + landed(take)
    step_grad[...] = value * temper

    for i, k in enumerate(sends):
        remote(mine(k), mine(k), ag_send.at[i], ag_mine.at[k], "side").wait_send()
    for i in range(len(LANDS)):
        remote(tx.at[i], rx.at[i], rs_send.at[i], rs_recv.at[i], "side").wait_send()
    for k in range(CHIPS):
        to_side(k).wait_send()


def hand_over(loss, grad, step_grad, loss_out, grad_out, step_grad_out, sem):
    copies = [
        pltpu.make_async_copy(grad, grad_out, sem.at[0]),
        pltpu.make_async_copy(step_grad, step_grad_out, sem.at[1]),
        pltpu.make_async_copy(loss, loss_out, sem.at[2]),
    ]
    for copy in copies:
        copy.start()
    for copy in copies:
        copy.wait()


def shards(frames, w_frame, step_emb, targets, tile_frame, tile_step, tile_count):
    n_frames, depth = frames.shape
    steps, width = step_emb.shape
    blocks = n_frames // BLK
    vmem = pl.BlockSpec(memory_space=pltpu.VMEM)
    anywhere = pl.BlockSpec(memory_space=pl.ANY)
    dma = pltpu.SemaphoreType.DMA
    results = (
        jax.ShapeDtypeStruct((blocks, BLK), F32),
        jax.ShapeDtypeStruct((n_frames, depth), BF16),
        jax.ShapeDtypeStruct((steps, width), F32),
    )
    held = tuple(pltpu.VMEM(r.shape, r.dtype) for r in results)
    found = pl.pallas_call(
        kernel,
        name="contrastive",
        out_shape=held,
        in_specs=[anywhere] * 7,
        out_specs=(vmem,) * 3,
        scratch_shapes=[
            pltpu.VMEM((n_frames, depth), BF16),
            pltpu.VMEM((depth, width), BF16),
            pltpu.VMEM((n_frames, width), BF16),
            pltpu.VMEM((CHIPS, 2 * BLK, width), BF16),
            pltpu.VMEM((width, LATE * 2 * BLK), BF16),
            pltpu.VMEM((width, BLK), BF16),
            pltpu.VMEM((CHIPS, 2 * BLK, n_frames), F32),
            pltpu.VMEM((CHIPS * 2 * BLK, n_frames), BF16),
            pltpu.VMEM((GROUP * 2 * BLK, n_frames), BF16),
            pltpu.VMEM((width, n_frames), F32),
            pltpu.VMEM((CHIPS, 2, n_frames), F32),
            pltpu.VMEM((1, n_frames), F32),
            pltpu.VMEM((1, n_frames), F32),
            pltpu.VMEM((1, n_frames), F32),
            pltpu.VMEM((BLK, n_frames), BF16),
            pltpu.VMEM((BLK, width), F32),
            pltpu.VMEM((2 * BLK, width), BF16),
            pltpu.VMEM((CHIPS, BLK, width), F32),
            pltpu.VMEM((CHIPS, BLK, width), BF16),
            pltpu.VMEM((CHIPS, BLK, width), BF16),
            pltpu.VMEM((len(LANDS), BLK, width), BF16),
            pltpu.VMEM((len(LANDS), BLK, width), BF16),
            pltpu.VMEM((width, n_frames), BF16),
            pltpu.VMEM((blocks, BLK), jnp.int32),
            pltpu.VMEM((1, BLK), jnp.int32),
            pltpu.VMEM((1, BLK), jnp.int32),
            pltpu.VMEM((1, 1), jnp.int32),
            dma((7,)),
            dma((31,)),
            dma((CHIPS,)),
            dma((CHIPS,)),
            dma((len(LANDS),)),
            dma((len(LANDS),)),
            dma((CHIPS,)),
            dma((CHIPS,)),
        ],
        compiler_params=pltpu.CompilerParams(
            collective_id=0, has_side_effects=True, vmem_limit_bytes=54 * 1024 * 1024
        ),
    )(
        step_emb, targets.reshape(blocks, BLK), tile_frame, tile_step,
        tile_count.reshape(1, 1), frames, w_frame,
    )
    loss, grad, step_grad = pl.pallas_call(
        hand_over,
        name="hand_over",
        out_shape=results,
        in_specs=[pl.BlockSpec(memory_space=pltpu.VMEM)] * 3,
        out_specs=(anywhere,) * 3,
        scratch_shapes=[dma((3,))],
    )(*[pltpu.with_memory_space_constraint(f, pltpu.VMEM) for f in found])
    return (loss.reshape(n_frames), grad, step_grad)


def solution(mesh):
    placed = (
        P(("grp", "vid"), None),
        P(),
        P(("grp", "vid"), None),
        P(("grp", "vid")),
        P(("grp", "vid"), None),
        P(("grp", "vid"), None),
        P(("grp", "vid")),
    )
    return jax.shard_map(
        shards,
        mesh=mesh,
        in_specs=placed,
        out_specs=(P(("grp", "vid")), P(("grp", "vid"), None), P(("grp", "vid"), None)),
        check_vma=False,
    )
```

```python
import functools
import math

import jax
import jax.numpy as jnp
from jax import lax
from jax.experimental import pallas as pl
from jax.experimental.pallas import tpu as pltpu
from jax.sharding import PartitionSpec as P

F32 = jnp.float32
BF16 = jnp.bfloat16
MESH = pl.DeviceIdType.MESH
NT = (((1,), (1,)), ((), ()))
SIDE = 4
CHIPS = SIDE * SIDE
BLK = 128
LOG2E = 1.0 / math.log(2.0)
LN2 = math.log(2.0)
FAR = -1e30

ORDER = [
    (0, 0), (0, 1), (1, 0), (0, 3), (3, 0), (1, 1), (3, 3), (1, 3),
    (3, 1), (2, 0), (0, 2), (2, 1), (1, 2), (2, 3), (3, 2), (2, 2),
]
POS = {place: k for k, place in enumerate(ORDER)}
TURN = [POS[(db, da)] for da, db in ORDER]

GATHER = {1: [(3, 0), (1, 0), (0, 3), (0, 1)], 2: [(2, 0)], 3: [(3, 3), (3, 1)], 4: [(1, 1), (1, 3)], 5: [(2, 1), (2, 3)], 7: [(0, 2)], 8: [(3, 2), (1, 2)], 11: [(2, 2)]}
ONWARD = {
    (0, 0): ['a+', 'a-', 'b+', 'b-', 'a2'],
    (3, 0): ["b+", "b-"],
    (1, 0): ["b+", "b-"],
    (2, 0): ["b+", "b-"],
    (0, 3): ["b+"],
    (1, 3): ["b+"],
    (2, 1): ["b-"],
    (3, 1): ["b-"],
}
SHIFT = {"a+": (-1, 0), "a-": (1, 0), "a2": (-2, 0), "b+": (0, -1), "b-": (0, 1), "b2": (0, -2)}

LANDS = ["h0", "h1", "h2", "h3", "p0", "p1", "p2", "p3",
         "m0", "m1", "m2", "m3", "A2", "Ap", "Am"]
LAND = {name: i for i, name in enumerate(LANDS)}
COMBINE = {
    (2, 2): ([], "b-", "h2"),
    (3, 2): ([], "b-", "h3"),
    (1, 2): ([], "b+", "h1"),
    (0, 2): ([], "b+", "h0"),
    (2, 3): (["h2"], "b-", "m2"),
    (3, 3): (["h3"], "b-", "m3"),
    (1, 3): ([], "b-", "m1"),
    (0, 3): ([], "b-", "m0"),
    (2, 1): ([], "b+", "p2"),
    (3, 1): ([], "b+", "p3"),
    (1, 1): (["h1"], "b+", "p1"),
    (0, 1): (["h0"], "b+", "p0"),
    (2, 0): (["p2", "m2"], "a2", "A2"),
    (1, 0): (["p1", "m1"], "a+", "Ap"),
    (3, 0): (["p3", "m3"], "a-", "Am"),
}
REDUCE = {
    4: [(2, 2)],
    6: [(3, 2)],
    8: [(2, 1), (1, 2)],
    10: [(0, 2)],
    12: [(3, 1), (1, 3), (2, 3)],
    13: [(3, 3)],
    14: [(1, 1)],
}
REDUCE_LATE = {(0, 0): [(0, 3)], (0, 1): [(0, 1), (2, 0)], (1, 0): [(3, 0), (1, 0)]}
EARLY = 4
LATE = CHIPS - EARLY
GROUP = 1


def kernel(
    step_hbm, tgt_hbm, tile_frame_hbm, tile_step_hbm, count_hbm, frames_hbm, w_hbm,
    loss, grad, step_grad,
    frames, w, emb, table, table_t, step_t, scores, probs, near, toward, bias, top, total,
    shift, onehot, own, turned_rows, part, side_tx, side_rx, tx, rx, emb_t,
    tgt, tile_frame, tile_step, count,
    load_sem, ag_send, ag_mine, ag_other, rs_send, rs_recv, side_send, side_recv,
):
    n_frames, width = emb.shape
    blocks = n_frames // BLK
    cols = 256
    pieces = n_frames // cols
    temper = 1.0 / math.sqrt(width)

    me = lax.axis_index("vid")
    core = me % 2
    z = (me // 2) % SIDE
    y = me // (2 * SIDE)

    def owner(da, db, other):
        ya = (y + da * (1 - core) + db * core) % SIDE
        zb = (z + db * (1 - core) + da * core) % SIDE
        kind = core + other * (1 - 2 * core)
        return (ya * SIDE + zb) * 2 + kind

    dev = {
        "a+": owner(1, 0, 0), "a-": owner(3, 0, 0), "a2": owner(2, 0, 0),
        "b+": owner(0, 1, 0), "b-": owner(0, 3, 0), "b2": owner(0, 2, 0),
        "side": owner(0, 0, 1),
    }

    barrier = pltpu.get_barrier_semaphore()
    for name in dev:
        pl.semaphore_signal(barrier, inc=1, device_id={"vid": dev[name]}, device_id_type=MESH)
    loads = [
        pltpu.make_async_copy(src, dst, load_sem.at[i])
        for i, (src, dst) in enumerate([
            (tile_frame_hbm, tile_frame), (tile_step_hbm, tile_step), (count_hbm, count),
            (tgt_hbm, tgt), (step_hbm, table.at[0, pl.ds(0, BLK)]),
            (frames_hbm, frames), (w_hbm, w),
        ])
    ]
    for load in loads:
        load.start()
    toward[...] = jnp.zeros_like(toward)
    for load in loads[:5]:
        load.wait()

    row = lax.broadcasted_iota(jnp.int32, (2 * CHIPS, BLK), 0)
    ids = jnp.zeros((2 * CHIPS, BLK), jnp.int32)
    for k, (da, db) in enumerate(ORDER):
        for other in range(2):
            ids = jnp.where(row == 2 * k + other, owner(da, db, other), ids)
    step_hot = jnp.where(ids == tile_step[...], 1.0, 0.0).astype(BF16)
    block_of = lax.broadcasted_iota(jnp.int32, (n_frames, BLK), 0) // BLK
    slot = lax.broadcasted_iota(jnp.int32, (n_frames, BLK), 1)
    frame_hot = jnp.where(
        (block_of == tile_frame[...]) & (slot < count[...]), 1.0, 0.0
    ).astype(BF16)
    seen = lax.dot_general(step_hot, frame_hot, NT, preferred_element_type=F32)
    hidden = jnp.where(seen > 0.5, 0.0, FAR)
    for k in range(CHIPS):
        bias[k] = hidden[2 * k : 2 * k + 2, :]
    label = lax.broadcasted_iota(jnp.int32, (BLK, BLK), 0)
    for b in range(blocks):
        onehot[:, b * BLK : (b + 1) * BLK] = jnp.where(
            label == tgt[b : b + 1, :], 1.0, 0.0
        ).astype(BF16)
    top[...] = jnp.full_like(top, FAR)
    total[...] = jnp.zeros_like(total)

    step_t[...] = table[0, 0:BLK, :].T
    pl.semaphore_wait(barrier, len(dev))

    def mine(k):
        return table.at[k, pl.ds(0, BLK)]

    def others(k):
        return table.at[k, pl.ds(BLK, BLK)]

    def remote(src, dst, send, recv, name):
        return pltpu.make_async_remote_copy(
            src_ref=src, dst_ref=dst, send_sem=send, recv_sem=recv,
            device_id={"vid": dev[name]}, device_id_type=MESH,
        )

    sends = []

    def pass_on(place):
        k = POS[place]
        for name in ONWARD.get(place, []):
            sa, sb = SHIFT[name]
            land = POS[((place[0] + sa) % SIDE, (place[1] + sb) % SIDE)]
            sends.append(k)
            remote(mine(k), mine(land), ag_send.at[len(sends) - 1], ag_mine.at[land], name).start()
        sends.append(k)
        remote(
            mine(k), others(TURN[k]), ag_send.at[len(sends) - 1], ag_other.at[TURN[k]], "side"
        ).start()

    def arrive(place):
        k = POS[place]
        remote(mine(k), mine(k), ag_send.at[0], ag_mine.at[k], "side").wait_recv()
        pass_on(place)

    pass_on((0, 0))

    for load in loads[5:]:
        load.wait()
    for n in range(pieces):
        rows = slice(n * cols, (n + 1) * cols)
        emb[rows, :] = jnp.dot(
            frames[rows, :], w[...], preferred_element_type=F32
        ).astype(BF16)
        emb_t[:, rows] = emb[rows, :].T

    def score(k, early):
        for step in GATHER:
            if (step * GROUP < EARLY) == early:
                @pl.when(k == step)
                def _():
                    for place in GATHER[step]:
                        arrive(place)
        tabs, turns = [], []
        for g in range(GROUP):
            j = k * GROUP + g
            remote(others(j), others(j), ag_send.at[0], ag_other.at[j], "side").wait_recv()
            tabs.append(table[j])
            turns.append(tabs[-1].T)
        tab = jnp.concatenate(tabs, axis=0)
        turned = jnp.concatenate(turns, axis=1)
        tall = 2 * BLK * GROUP
        if not early:
            base = pl.multiple_of((k * GROUP - EARLY) * 2 * BLK, tall)
            table_t[:, pl.ds(base, tall)] = turned
        for n in range(pieces):
            fs = slice(n * cols, (n + 1) * cols)
            raw = jnp.dot(tab, emb_t[:, fs], preferred_element_type=F32)
            parts = []
            before = top[:, fs]
            after = before
            for g in range(2 * GROUP):
                j, h = g // 2, g % 2
                value = raw[g * BLK : (g + 1) * BLK] * (temper * LOG2E) + bias[
                    k * GROUP + j, h : h + 1, fs
                ]
                scores[k * GROUP + j, h * BLK : (h + 1) * BLK, fs] = value
                after = jnp.maximum(after, jnp.max(value, axis=0, keepdims=True))
                parts.append(value)
            fade = jnp.exp2(before - after)
            gained = total[:, fs] * fade
            for g in range(2 * GROUP):
                value = jnp.exp2(parts[g] - after)
                gained = gained + jnp.sum(value, axis=0, keepdims=True)
                if early:
                    near[g * BLK : (g + 1) * BLK, fs] = value.astype(BF16)
            total[:, fs] = gained
            top[:, fs] = after
            if early:
                toward[:, fs] = toward[:, fs] * fade + jnp.dot(
                    turned, near[:, fs], preferred_element_type=F32
                )

    @pl.loop(0, EARLY // GROUP)
    def _(k):
        score(k, True)

    shift[...] = top[...]

    @pl.loop(EARLY // GROUP, CHIPS // GROUP)
    def _(k):
        score(k, False)

    lse = top[...] + jnp.log(total[...]) * LOG2E
    top[...] = jnp.exp2(shift[...] - lse)
    shift[...] = lse
    for b in range(blocks):
        fs = slice(b * BLK, (b + 1) * BLK)
        kept = jnp.where(label == tgt[b : b + 1, :], scores[0, 0:BLK, fs], 0.0)
        positive = jnp.sum(kept, axis=0, keepdims=True)
        loss[b : b + 1, :] = (shift[:, fs] - positive) * LN2

    def landed(name):
        i = LAND[name]
        remote(rx.at[i], rx.at[i], ag_send.at[0], rs_recv.at[i], "side").wait_recv()
        return rx[i].astype(F32)

    def gathered(place):
        k = POS[place]
        remote(side_rx.at[k], side_rx.at[k], ag_send.at[0], side_recv.at[k], "side").wait_recv()
        return part[k] + side_rx[k].astype(F32)

    def combine(place):
        takes, name, land = COMBINE[place]
        value = gathered(place)
        for take in takes:
            value = value + landed(take)
        i = LAND[land]
        tx[i] = value.astype(BF16)
        remote(tx.at[i], rx.at[i], rs_send.at[i], rs_recv.at[i], name).start()

    def to_side(k):
        return remote(
            side_tx.at[k], side_rx.at[TURN[k]], side_send.at[k], side_recv.at[TURN[k]], "side"
        )

    @pl.loop(0, CHIPS // 2)
    def _(i):
        k = CHIPS - 2 - 2 * i
        tall = 4 * BLK
        base = pl.multiple_of(k * 2 * BLK, tall)
        for n in range(pieces):
            fs = slice(n * cols, (n + 1) * cols)
            for g in range(2):
                probs[pl.ds(base + g * 2 * BLK, 2 * BLK), fs] = jnp.exp2(
                    scores[k + g, :, fs] - shift[:, fs]
                ).astype(BF16)
        out = jnp.dot(probs[pl.ds(base, tall), :], emb[...], preferred_element_type=F32)
        for g in range(2):
            part[k + g] = out[2 * g * BLK : (2 * g + 1) * BLK]
            side_tx[k + g] = out[(2 * g + 1) * BLK : (2 * g + 2) * BLK].astype(BF16)
        for step in range(CHIPS // 2):
            @pl.when(i == step)
            def _():
                to_side(CHIPS - 1 - 2 * step).start()
                to_side(CHIPS - 2 - 2 * step).start()
                for place in REDUCE.get(2 * step, []) + REDUCE.get(2 * step + 1, []):
                    combine(place)

    own[...] = jnp.dot(onehot[...], emb[...], preferred_element_type=F32)

    @pl.loop(0, pieces // 2)
    def _(n):
        for (piece, half), places in REDUCE_LATE.items():
            if half == 0:
                @pl.when(n == piece)
                def _():
                    for place in places:
                        combine(place)
        fs = pl.ds(pl.multiple_of(n * 2 * cols, 2 * cols), 2 * cols)
        rows = toward[:, fs] * top[:, fs] - jnp.dot(
            step_t[...], onehot[:, fs], preferred_element_type=F32
        )
        rows = rows + jnp.dot(
            table_t[...], probs[EARLY * 2 * BLK :, fs], preferred_element_type=F32
        )
        rows_t = (rows * temper).astype(BF16).T
        turned_rows[...] = rows_t
        for (piece, half), places in REDUCE_LATE.items():
            if half == 1:
                @pl.when(n == piece)
                def _():
                    for place in places:
                        combine(place)
        grad[fs, :] = lax.dot_general(
            turned_rows[...], w[...], NT, preferred_element_type=F32
        ).astype(BF16)

    value = gathered((0, 0)) - own[...]
    for take in ["p0", "m0", "Am", "A2", "Ap"]:
        value = value + landed(take)
    step_grad[...] = value * temper

    for i, k in enumerate(sends):
        remote(mine(k), mine(k), ag_send.at[i], ag_mine.at[k], "side").wait_send()
    for i in range(len(LANDS)):
        remote(tx.at[i], rx.at[i], rs_send.at[i], rs_recv.at[i], "side").wait_send()
    for k in range(CHIPS):
        to_side(k).wait_send()


def hand_over(loss, grad, step_grad, loss_out, grad_out, step_grad_out, sem):
    copies = [
        pltpu.make_async_copy(grad, grad_out, sem.at[0]),
        pltpu.make_async_copy(step_grad, step_grad_out, sem.at[1]),
        pltpu.make_async_copy(loss, loss_out, sem.at[2]),
    ]
    for copy in copies:
        copy.start()
    for copy in copies:
        copy.wait()


def shards(frames, w_frame, step_emb, targets, tile_frame, tile_step, tile_count):
    n_frames, depth = frames.shape
    steps, width = step_emb.shape
    blocks = n_frames // BLK
    vmem = pl.BlockSpec(memory_space=pltpu.VMEM)
    anywhere = pl.BlockSpec(memory_space=pl.ANY)
    dma = pltpu.SemaphoreType.DMA
    results = (
        jax.ShapeDtypeStruct((blocks, BLK), F32),
        jax.ShapeDtypeStruct((n_frames, depth), BF16),
        jax.ShapeDtypeStruct((steps, width), F32),
    )
    held = tuple(pltpu.VMEM(r.shape, r.dtype) for r in results)
    found = pl.pallas_call(
        kernel,
        name="contrastive",
        out_shape=held,
        in_specs=[anywhere] * 7,
        out_specs=(vmem,) * 3,
        scratch_shapes=[
            pltpu.VMEM((n_frames, depth), BF16),
            pltpu.VMEM((depth, width), BF16),
            pltpu.VMEM((n_frames, width), BF16),
            pltpu.VMEM((CHIPS, 2 * BLK, width), BF16),
            pltpu.VMEM((width, LATE * 2 * BLK), BF16),
            pltpu.VMEM((width, BLK), BF16),
            pltpu.VMEM((CHIPS, 2 * BLK, n_frames), F32),
            pltpu.VMEM((CHIPS * 2 * BLK, n_frames), BF16),
            pltpu.VMEM((GROUP * 2 * BLK, n_frames), BF16),
            pltpu.VMEM((width, n_frames), F32),
            pltpu.VMEM((CHIPS, 2, n_frames), F32),
            pltpu.VMEM((1, n_frames), F32),
            pltpu.VMEM((1, n_frames), F32),
            pltpu.VMEM((1, n_frames), F32),
            pltpu.VMEM((BLK, n_frames), BF16),
            pltpu.VMEM((BLK, width), F32),
            pltpu.VMEM((4 * BLK, width), BF16),
            pltpu.VMEM((CHIPS, BLK, width), F32),
            pltpu.VMEM((CHIPS, BLK, width), BF16),
            pltpu.VMEM((CHIPS, BLK, width), BF16),
            pltpu.VMEM((len(LANDS), BLK, width), BF16),
            pltpu.VMEM((len(LANDS), BLK, width), BF16),
            pltpu.VMEM((width, n_frames), BF16),
            pltpu.VMEM((blocks, BLK), jnp.int32),
            pltpu.VMEM((1, BLK), jnp.int32),
            pltpu.VMEM((1, BLK), jnp.int32),
            pltpu.VMEM((1, 1), jnp.int32),
            dma((7,)),
            dma((31,)),
            dma((CHIPS,)),
            dma((CHIPS,)),
            dma((len(LANDS),)),
            dma((len(LANDS),)),
            dma((CHIPS,)),
            dma((CHIPS,)),
        ],
        compiler_params=pltpu.CompilerParams(
            collective_id=0, has_side_effects=True, vmem_limit_bytes=54 * 1024 * 1024
        ),
    )(
        step_emb, targets.reshape(blocks, BLK), tile_frame, tile_step,
        tile_count.reshape(1, 1), frames, w_frame,
    )
    loss, grad, step_grad = pl.pallas_call(
        hand_over,
        name="hand_over",
        out_shape=results,
        in_specs=[pl.BlockSpec(memory_space=pltpu.VMEM)] * 3,
        out_specs=(anywhere,) * 3,
        scratch_shapes=[dma((3,))],
    )(*[pltpu.with_memory_space_constraint(f, pltpu.VMEM) for f in found])
    return (loss.reshape(n_frames), grad, step_grad)


def solution(mesh):
    placed = (
        P(("grp", "vid"), None),
        P(),
        P(("grp", "vid"), None),
        P(("grp", "vid")),
        P(("grp", "vid"), None),
        P(("grp", "vid"), None),
        P(("grp", "vid")),
    )
    return jax.shard_map(
        shards,
        mesh=mesh,
        in_specs=placed,
        out_specs=(P(("grp", "vid")), P(("grp", "vid"), None), P(("grp", "vid"), None)),
        check_vma=False,
    )
```

```python
import functools
import math

import jax
import jax.numpy as jnp
from jax import lax
from jax.experimental import pallas as pl
from jax.experimental.pallas import tpu as pltpu
from jax.sharding import PartitionSpec as P

F32 = jnp.float32
BF16 = jnp.bfloat16
MESH = pl.DeviceIdType.MESH
NT = (((1,), (1,)), ((), ()))
SIDE = 4
CHIPS = SIDE * SIDE
BLK = 128
LOG2E = 1.0 / math.log(2.0)
LN2 = math.log(2.0)
FAR = -1e30

ORDER = [
    (0, 0), (0, 1), (1, 0), (0, 3), (3, 0), (1, 1), (3, 3), (1, 3),
    (3, 1), (2, 0), (0, 2), (2, 1), (1, 2), (2, 3), (3, 2), (2, 2),
]
POS = {place: k for k, place in enumerate(ORDER)}
TURN = [POS[(db, da)] for da, db in ORDER]

GATHER = {1: [(3, 0), (1, 0), (0, 3), (0, 1)], 2: [(2, 0)], 3: [(3, 3), (3, 1)], 4: [(1, 1), (1, 3)], 5: [(2, 1), (2, 3)], 7: [(0, 2)], 8: [(3, 2), (1, 2)], 12: [(2, 2)]}
ONWARD = {
    (0, 0): ['a+', 'a-', 'b+', 'b-', 'a2'],
    (3, 0): ["b+", "b-"],
    (1, 0): ["b+", "b-"],
    (2, 0): ["b+", "b-"],
    (0, 3): ["b+"],
    (1, 3): ["b+"],
    (2, 1): ["b-"],
    (3, 1): ["b-"],
}
SHIFT = {"a+": (-1, 0), "a-": (1, 0), "a2": (-2, 0), "b+": (0, -1), "b-": (0, 1), "b2": (0, -2)}

LANDS = ["h0", "h1", "h2", "h3", "p0", "p1", "p2", "p3",
         "m0", "m1", "m2", "m3", "A2", "Ap", "Am"]
LAND = {name: i for i, name in enumerate(LANDS)}
COMBINE = {
    (2, 2): ([], "b-", "h2"),
    (3, 2): ([], "b-", "h3"),
    (1, 2): ([], "b+", "h1"),
    (0, 2): ([], "b+", "h0"),
    (2, 3): (["h2"], "b-", "m2"),
    (3, 3): (["h3"], "b-", "m3"),
    (1, 3): ([], "b-", "m1"),
    (0, 3): ([], "b-", "m0"),
    (2, 1): ([], "b+", "p2"),
    (3, 1): ([], "b+", "p3"),
    (1, 1): (["h1"], "b+", "p1"),
    (0, 1): (["h0"], "b+", "p0"),
    (2, 0): (["p2", "m2"], "a2", "A2"),
    (1, 0): (["p1", "m1"], "a+", "Ap"),
    (3, 0): (["p3", "m3"], "a-", "Am"),
}
REDUCE = {
    4: [(2, 2)],
    6: [(3, 2)],
    8: [(2, 1), (1, 2)],
    10: [(0, 2)],
    12: [(3, 1), (1, 3), (2, 3)],
    13: [(3, 3)],
    14: [(1, 1)],
}
REDUCE_LATE = {(0, 0): [(0, 3)], (0, 1): [(0, 1), (2, 0)], (1, 0): [(3, 0), (1, 0)]}
EARLY = 4
LATE = CHIPS - EARLY
PAIRED = 8


def kernel(
    step_hbm, tgt_hbm, tile_frame_hbm, tile_step_hbm, count_hbm, frames_hbm, w_hbm,
    loss, grad, step_grad,
    frames, w, emb, table, table_t, step_t, scores, probs, near, toward, bias, top, total,
    shift, onehot, own, turned_rows, part, side_tx, side_rx, tx, rx, emb_t,
    tgt, tile_frame, tile_step, count,
    load_sem, ag_send, ag_mine, ag_other, rs_send, rs_recv, side_send, side_recv,
):
    n_frames, width = emb.shape
    blocks = n_frames // BLK
    cols = 256
    pieces = n_frames // cols
    temper = 1.0 / math.sqrt(width)

    me = lax.axis_index("vid")
    core = me % 2
    z = (me // 2) % SIDE
    y = me // (2 * SIDE)

    def owner(da, db, other):
        ya = (y + da * (1 - core) + db * core) % SIDE
        zb = (z + db * (1 - core) + da * core) % SIDE
        kind = core + other * (1 - 2 * core)
        return (ya * SIDE + zb) * 2 + kind

    dev = {
        "a+": owner(1, 0, 0), "a-": owner(3, 0, 0), "a2": owner(2, 0, 0),
        "b+": owner(0, 1, 0), "b-": owner(0, 3, 0), "b2": owner(0, 2, 0),
        "side": owner(0, 0, 1),
    }

    barrier = pltpu.get_barrier_semaphore()
    for name in dev:
        pl.semaphore_signal(barrier, inc=1, device_id={"vid": dev[name]}, device_id_type=MESH)
    loads = [
        pltpu.make_async_copy(src, dst, load_sem.at[i])
        for i, (src, dst) in enumerate([
            (tile_frame_hbm, tile_frame), (tile_step_hbm, tile_step), (count_hbm, count),
            (tgt_hbm, tgt), (step_hbm, table.at[0, pl.ds(0, BLK)]),
            (frames_hbm, frames), (w_hbm, w),
        ])
    ]
    for load in loads:
        load.start()
    toward[...] = jnp.zeros_like(toward)
    for load in loads[:5]:
        load.wait()

    row = lax.broadcasted_iota(jnp.int32, (2 * CHIPS, BLK), 0)
    ids = jnp.zeros((2 * CHIPS, BLK), jnp.int32)
    for k, (da, db) in enumerate(ORDER):
        for other in range(2):
            ids = jnp.where(row == 2 * k + other, owner(da, db, other), ids)
    step_hot = jnp.where(ids == tile_step[...], 1.0, 0.0).astype(BF16)
    block_of = lax.broadcasted_iota(jnp.int32, (n_frames, BLK), 0) // BLK
    slot = lax.broadcasted_iota(jnp.int32, (n_frames, BLK), 1)
    frame_hot = jnp.where(
        (block_of == tile_frame[...]) & (slot < count[...]), 1.0, 0.0
    ).astype(BF16)
    seen = lax.dot_general(step_hot, frame_hot, NT, preferred_element_type=F32)
    hidden = jnp.where(seen > 0.5, 0.0, FAR)
    for k in range(CHIPS):
        bias[k] = hidden[2 * k : 2 * k + 2, :]
    label = lax.broadcasted_iota(jnp.int32, (BLK, BLK), 0)
    for b in range(blocks):
        onehot[:, b * BLK : (b + 1) * BLK] = jnp.where(
            label == tgt[b : b + 1, :], 1.0, 0.0
        ).astype(BF16)
    top[...] = jnp.full_like(top, FAR)
    total[...] = jnp.zeros_like(total)

    step_t[...] = table[0, 0:BLK, :].T
    pl.semaphore_wait(barrier, len(dev))

    def mine(k):
        return table.at[k, pl.ds(0, BLK)]

    def others(k):
        return table.at[k, pl.ds(BLK, BLK)]

    def remote(src, dst, send, recv, name):
        return pltpu.make_async_remote_copy(
            src_ref=src, dst_ref=dst, send_sem=send, recv_sem=recv,
            device_id={"vid": dev[name]}, device_id_type=MESH,
        )

    sends = []

    def pass_on(place):
        k = POS[place]
        for name in ONWARD.get(place, []):
            sa, sb = SHIFT[name]
            land = POS[((place[0] + sa) % SIDE, (place[1] + sb) % SIDE)]
            sends.append(k)
            remote(mine(k), mine(land), ag_send.at[len(sends) - 1], ag_mine.at[land], name).start()
        sends.append(k)
        remote(
            mine(k), others(TURN[k]), ag_send.at[len(sends) - 1], ag_other.at[TURN[k]], "side"
        ).start()

    def arrive(place):
        k = POS[place]
        remote(mine(k), mine(k), ag_send.at[0], ag_mine.at[k], "side").wait_recv()
        pass_on(place)

    pass_on((0, 0))

    for load in loads[5:]:
        load.wait()
    for n in range(pieces):
        rows = slice(n * cols, (n + 1) * cols)
        emb[rows, :] = jnp.dot(
            frames[rows, :], w[...], preferred_element_type=F32
        ).astype(BF16)
        emb_t[:, rows] = emb[rows, :].T

    def score(k, first, last, group):
        early = last <= EARLY
        for step in GATHER:
            if first <= step < last:
                @pl.when(k * group == step)
                def _():
                    for place in GATHER[step]:
                        arrive(place)
        tabs, turns = [], []
        for g in range(group):
            j = k * group + g
            remote(others(j), others(j), ag_send.at[0], ag_other.at[j], "side").wait_recv()
            tabs.append(table[j])
            turns.append(tabs[-1].T)
        tab = jnp.concatenate(tabs, axis=0)
        turned = jnp.concatenate(turns, axis=1)
        tall = 2 * BLK * group
        if not early:
            base = pl.multiple_of((k * group - EARLY) * 2 * BLK, tall)
            table_t[:, pl.ds(base, tall)] = turned
        for n in range(pieces):
            fs = slice(n * cols, (n + 1) * cols)
            raw = jnp.dot(tab, emb_t[:, fs], preferred_element_type=F32)
            parts = []
            before = top[:, fs]
            after = before
            for g in range(2 * group):
                j, h = g // 2, g % 2
                value = raw[g * BLK : (g + 1) * BLK] * (temper * LOG2E) + bias[
                    k * group + j, h : h + 1, fs
                ]
                scores[k * group + j, h * BLK : (h + 1) * BLK, fs] = value
                after = jnp.maximum(after, jnp.max(value, axis=0, keepdims=True))
                parts.append(value)
            fade = jnp.exp2(before - after)
            gained = total[:, fs] * fade
            for g in range(2 * group):
                value = jnp.exp2(parts[g] - after)
                gained = gained + jnp.sum(value, axis=0, keepdims=True)
                if early:
                    near[g * BLK : (g + 1) * BLK, fs] = value.astype(BF16)
            total[:, fs] = gained
            top[:, fs] = after
            if early:
                toward[:, fs] = toward[:, fs] * fade + jnp.dot(
                    turned, near[:, fs], preferred_element_type=F32
                )

    @pl.loop(0, EARLY)
    def _(k):
        score(k, 0, EARLY, 1)

    shift[...] = top[...]

    @pl.loop(EARLY, PAIRED)
    def _(k):
        score(k, EARLY, PAIRED, 1)

    @pl.loop(PAIRED // 2, CHIPS // 2)
    def _(k):
        score(k, PAIRED, CHIPS, 2)

    lse = top[...] + jnp.log(total[...]) * LOG2E
    top[...] = jnp.exp2(shift[...] - lse)
    shift[...] = lse
    for b in range(blocks):
        fs = slice(b * BLK, (b + 1) * BLK)
        kept = jnp.where(label == tgt[b : b + 1, :], scores[0, 0:BLK, fs], 0.0)
        positive = jnp.sum(kept, axis=0, keepdims=True)
        loss[b : b + 1, :] = (shift[:, fs] - positive) * LN2

    def landed(name):
        i = LAND[name]
        remote(rx.at[i], rx.at[i], ag_send.at[0], rs_recv.at[i], "side").wait_recv()
        return rx[i].astype(F32)

    def gathered(place):
        k = POS[place]
        remote(side_rx.at[k], side_rx.at[k], ag_send.at[0], side_recv.at[k], "side").wait_recv()
        return part[k] + side_rx[k].astype(F32)

    def combine(place):
        takes, name, land = COMBINE[place]
        value = gathered(place)
        for take in takes:
            value = value + landed(take)
        i = LAND[land]
        tx[i] = value.astype(BF16)
        remote(tx.at[i], rx.at[i], rs_send.at[i], rs_recv.at[i], name).start()

    def to_side(k):
        return remote(
            side_tx.at[k], side_rx.at[TURN[k]], side_send.at[k], side_recv.at[TURN[k]], "side"
        )

    @pl.loop(0, CHIPS // 2)
    def _(i):
        k = CHIPS - 2 - 2 * i
        tall = 4 * BLK
        base = pl.multiple_of(k * 2 * BLK, tall)
        for n in range(pieces):
            fs = slice(n * cols, (n + 1) * cols)
            for g in range(2):
                probs[pl.ds(base + g * 2 * BLK, 2 * BLK), fs] = jnp.exp2(
                    scores[k + g, :, fs] - shift[:, fs]
                ).astype(BF16)
        out = jnp.dot(probs[pl.ds(base, tall), :], emb[...], preferred_element_type=F32)
        for g in range(2):
            part[k + g] = out[2 * g * BLK : (2 * g + 1) * BLK]
            side_tx[k + g] = out[(2 * g + 1) * BLK : (2 * g + 2) * BLK].astype(BF16)
        for step in range(CHIPS // 2):
            @pl.when(i == step)
            def _():
                to_side(CHIPS - 1 - 2 * step).start()
                to_side(CHIPS - 2 - 2 * step).start()
                for place in REDUCE.get(2 * step, []) + REDUCE.get(2 * step + 1, []):
                    combine(place)

    own[...] = jnp.dot(onehot[...], emb[...], preferred_element_type=F32)

    @pl.loop(0, pieces // 2)
    def _(n):
        for (piece, half), places in REDUCE_LATE.items():
            if half == 0:
                @pl.when(n == piece)
                def _():
                    for place in places:
                        combine(place)
        fs = pl.ds(pl.multiple_of(n * 2 * cols, 2 * cols), 2 * cols)
        rows = toward[:, fs] * top[:, fs] - jnp.dot(
            step_t[...], onehot[:, fs], preferred_element_type=F32
        )
        rows = rows + jnp.dot(
            table_t[...], probs[EARLY * 2 * BLK :, fs], preferred_element_type=F32
        )
        rows_t = (rows * temper).astype(BF16).T
        turned_rows[...] = rows_t
        for (piece, half), places in REDUCE_LATE.items():
            if half == 1:
                @pl.when(n == piece)
                def _():
                    for place in places:
                        combine(place)
        grad[fs, :] = lax.dot_general(
            turned_rows[...], w[...], NT, preferred_element_type=F32
        ).astype(BF16)

    value = gathered((0, 0)) - own[...]
    for take in ["p0", "m0", "Am", "A2", "Ap"]:
        value = value + landed(take)
    step_grad[...] = value * temper

    for i, k in enumerate(sends):
        remote(mine(k), mine(k), ag_send.at[i], ag_mine.at[k], "side").wait_send()
    for i in range(len(LANDS)):
        remote(tx.at[i], rx.at[i], rs_send.at[i], rs_recv.at[i], "side").wait_send()
    for k in range(CHIPS):
        to_side(k).wait_send()


def hand_over(loss, grad, step_grad, loss_out, grad_out, step_grad_out, sem):
    copies = [
        pltpu.make_async_copy(grad, grad_out, sem.at[0]),
        pltpu.make_async_copy(step_grad, step_grad_out, sem.at[1]),
        pltpu.make_async_copy(loss, loss_out, sem.at[2]),
    ]
    for copy in copies:
        copy.start()
    for copy in copies:
        copy.wait()


def shards(frames, w_frame, step_emb, targets, tile_frame, tile_step, tile_count):
    n_frames, depth = frames.shape
    steps, width = step_emb.shape
    blocks = n_frames // BLK
    vmem = pl.BlockSpec(memory_space=pltpu.VMEM)
    anywhere = pl.BlockSpec(memory_space=pl.ANY)
    dma = pltpu.SemaphoreType.DMA
    results = (
        jax.ShapeDtypeStruct((blocks, BLK), F32),
        jax.ShapeDtypeStruct((n_frames, depth), BF16),
        jax.ShapeDtypeStruct((steps, width), F32),
    )
    held = tuple(pltpu.VMEM(r.shape, r.dtype) for r in results)
    found = pl.pallas_call(
        kernel,
        name="contrastive",
        out_shape=held,
        in_specs=[anywhere] * 7,
        out_specs=(vmem,) * 3,
        scratch_shapes=[
            pltpu.VMEM((n_frames, depth), BF16),
            pltpu.VMEM((depth, width), BF16),
            pltpu.VMEM((n_frames, width), BF16),
            pltpu.VMEM((CHIPS, 2 * BLK, width), BF16),
            pltpu.VMEM((width, LATE * 2 * BLK), BF16),
            pltpu.VMEM((width, BLK), BF16),
            pltpu.VMEM((CHIPS, 2 * BLK, n_frames), F32),
            pltpu.VMEM((CHIPS * 2 * BLK, n_frames), BF16),
            pltpu.VMEM((2 * BLK, n_frames), BF16),
            pltpu.VMEM((width, n_frames), F32),
            pltpu.VMEM((CHIPS, 2, n_frames), F32),
            pltpu.VMEM((1, n_frames), F32),
            pltpu.VMEM((1, n_frames), F32),
            pltpu.VMEM((1, n_frames), F32),
            pltpu.VMEM((BLK, n_frames), BF16),
            pltpu.VMEM((BLK, width), F32),
            pltpu.VMEM((4 * BLK, width), BF16),
            pltpu.VMEM((CHIPS, BLK, width), F32),
            pltpu.VMEM((CHIPS, BLK, width), BF16),
            pltpu.VMEM((CHIPS, BLK, width), BF16),
            pltpu.VMEM((len(LANDS), BLK, width), BF16),
            pltpu.VMEM((len(LANDS), BLK, width), BF16),
            pltpu.VMEM((width, n_frames), BF16),
            pltpu.VMEM((blocks, BLK), jnp.int32),
            pltpu.VMEM((1, BLK), jnp.int32),
            pltpu.VMEM((1, BLK), jnp.int32),
            pltpu.VMEM((1, 1), jnp.int32),
            dma((7,)),
            dma((31,)),
            dma((CHIPS,)),
            dma((CHIPS,)),
            dma((len(LANDS),)),
            dma((len(LANDS),)),
            dma((CHIPS,)),
            dma((CHIPS,)),
        ],
        compiler_params=pltpu.CompilerParams(
            collective_id=0, has_side_effects=True, vmem_limit_bytes=54 * 1024 * 1024
        ),
    )(
        step_emb, targets.reshape(blocks, BLK), tile_frame, tile_step,
        tile_count.reshape(1, 1), frames, w_frame,
    )
    loss, grad, step_grad = pl.pallas_call(
        hand_over,
        name="hand_over",
        out_shape=results,
        in_specs=[pl.BlockSpec(memory_space=pltpu.VMEM)] * 3,
        out_specs=(anywhere,) * 3,
        scratch_shapes=[dma((3,))],
    )(*[pltpu.with_memory_space_constraint(f, pltpu.VMEM) for f in found])
    return (loss.reshape(n_frames), grad, step_grad)


def solution(mesh):
    placed = (
        P(("grp", "vid"), None),
        P(),
        P(("grp", "vid"), None),
        P(("grp", "vid")),
        P(("grp", "vid"), None),
        P(("grp", "vid"), None),
        P(("grp", "vid")),
    )
    return jax.shard_map(
        shards,
        mesh=mesh,
        in_specs=placed,
        out_specs=(P(("grp", "vid")), P(("grp", "vid"), None), P(("grp", "vid"), None)),
        check_vma=False,
    )
```
